128 devices in a mesh: rcv: 16 (over x_hi, y, core), src: 8 (over z, x_lo).
Axes of the slice: x: 4 (x_hi: 2, x_lo: 2; x = x_hi * 2 + x_lo), y: 4, z: 4, core: 2. Of those that a mesh axis runs over, the one named last changes fastest.
Arguments:
- kernel_codes: bfloat16 [2, 8192, 65536], P(None, 'rcv', 'src'), may hold values from -128 to 127
- kernel_exps: int32 [8192, 512], P('rcv', 'src'), may hold values from -17 to -14
- wavefield: bfloat16 [2, 65536, 128], P(None, 'src', 'rcv'), may hold values from -6 to 6
- observed: bfloat16 [2, 8192, 128], P(None, 'rcv'), may hold values from -6 to 6
- receiver_mask: int32 [8192], P('rcv'), may hold values 0 or 1
Outputs:
- residual: bfloat16 [2, 8192, 128], P(None, 'rcv', 'src')
- gradient: bfloat16 [2, 65536, 128], P(None, 'src', 'rcv')
The draws below stay inside these ranges and needn't reach their ends.
All inputs are finite; a program needn't handle non-finite values. No bound on the sum of `receiver_mask` on one device may be relied on, other than what follows from the above.
Results may differ from the reference program's by a relative error of at most 0.0049.
Values may be sent and summed in bfloat16 or wider, within the bound.
No kernel may reach another device: no remote copies, remote signals or barrier semaphores. Data moves between devices by JAX's collectives and lax.ppermute only.
A program may use at most 128 MiB of HBM per device.

```python
import jax
import jax.numpy as jnp
from jax import lax

VIRT = 128
EXP_BLOCK = 128
NR = 8192
NS = 65536
N_RCV = 16


def draw_kernel_codes(key, part):
    whole = jax.random.randint(key, (2, NR, NS), -128, 128, dtype=jnp.int32)
    return whole.astype(jnp.float32).astype(jnp.bfloat16)


def set_ends(drawn, stream_key, low, top_value):
    extent = drawn.shape
    place = [jax.random.randint(jax.random.fold_in(stream_key, axis), (), 0, extent[axis]) for axis in range(len(extent))]
    drawn = drawn.at[tuple(place)].set(low)
    longest = extent.index(max(extent))
    place[longest] = (place[longest] + 1) % extent[longest]
    return drawn.at[tuple(place)].set(top_value)


def level_of(rng, shape, split, least, largest):
    factor_of, own = 1.0, jax.random.fold_in(rng, 6)
    for axis_at, blocks in split:
        steps = jnp.exp(jax.random.uniform(jax.random.fold_in(own, axis_at), (blocks,), jnp.float32, least / len(split), largest / len(split)))
        factor_of = factor_of * jnp.repeat(steps, shape[axis_at] // blocks).reshape([-1 if axis == axis_at else 1 for axis in range(len(shape))])
    return factor_of


def noise(rng, extent, spread, most, split=(), kind=jnp.bfloat16):
    loudness = level_of(rng, extent, split, -0.22, 0.18) if split else 1.0
    array = jax.random.normal(rng, extent, jnp.float32) * spread * loudness
    return jnp.minimum(jnp.maximum(array, -most), most).astype(kind)


def setup_inputs(seed: int = 0) -> dict:
    key_of = jax.random.split(jax.random.key(seed), 6)
    return {
        "kernel_codes": draw_kernel_codes(jax.random.fold_in(key_of[5], 71), 0),
        "kernel_exps": set_ends(jax.random.randint(key_of[1], (NR, NS // EXP_BLOCK), -17, -13), jax.random.fold_in(key_of[1], 1), -17, (-13) - 1).astype(jnp.int32),
        "wavefield": noise(key_of[2], (2, NS, VIRT), 1.0, 6.0, ((1, 8), (2, 16))),
        "observed": noise(key_of[3], (2, NR, VIRT), 1.0, 6.0, ((1, 16),)),
        "receiver_mask": set_ends((jax.random.randint(key_of[4], (NR,), 0, 4) < 3).astype(jnp.int32), jax.random.fold_in(key_of[4], 1), 0, 1),
    }


def decode(codes, exps):
    rows = codes.shape[1]
    cols = codes.shape[2]
    scale = jnp.exp2(exps.astype(jnp.float32))[:, :, None]

    def widen(values):
        blocks = values.reshape(rows, cols // EXP_BLOCK, EXP_BLOCK).astype(jnp.float32) * scale
        return blocks.reshape(rows, cols).astype(jnp.bfloat16)

    return jnp.concatenate([widen(codes[0]), widen(codes[1])], axis=0)


def reference(kernel_codes, kernel_exps, wavefield, observed, receiver_mask):
    rows = NR // N_RCV
    nblocks = NR // rows
    width = wavefield.shape[2]
    stacked_waves = jnp.concatenate([wavefield[0], wavefield[1]], axis=1)

    def one_block(carry, index):
        start = (index * rows).astype(jnp.int32)
        codes = lax.dynamic_slice_in_dim(kernel_codes, start, rows, 1)
        exps = lax.dynamic_slice_in_dim(kernel_exps, start, rows, 0)
        stacked = decode(codes, exps)
        prod = jnp.dot(stacked, stacked_waves, preferred_element_type=jnp.float32)
        pred_real = prod[:rows, :width] - prod[rows:, width:]
        pred_imag = prod[:rows, width:] + prod[rows:, :width]
        seen = lax.dynamic_slice_in_dim(observed, start, rows, 1).astype(jnp.float32)
        live = lax.dynamic_slice_in_dim(receiver_mask, start, rows, 0).astype(jnp.float32)[:, None]
        res_real = (live * (pred_real - seen[0])).astype(jnp.bfloat16)
        res_imag = (live * (pred_imag - seen[1])).astype(jnp.bfloat16)
        left = jnp.concatenate([res_real, res_imag], axis=0)
        right = jnp.concatenate([res_imag, -res_real], axis=0)
        bmat = jnp.concatenate([left, right], axis=1)
        term = lax.dot_general(stacked, bmat, (((0,), (0,)), ((), ())), preferred_element_type=jnp.float32)
        return carry + term, jnp.stack([res_real, res_imag])

    init = jnp.zeros((NS, 2 * width), jnp.float32)
    total, pieces = lax.scan(one_block, init, jnp.arange(nblocks, dtype=jnp.int32))
    residual = jnp.transpose(pieces, (1, 0, 2, 3)).reshape(2, NR, width)
    gradient = jnp.stack([total[:, :width], total[:, width:]]).astype(jnp.bfloat16)
    return residual, gradient
```

```python
import jax
import jax.numpy as jnp
from jax import lax
from jax.experimental import pallas as pl
from jax.experimental.pallas import tpu as pltpu
from jax.sharding import Mesh, PartitionSpec as P

EXP_BLOCK = 128
XY = ("xh", "y")
RCV = ("xh", "y", "c")
SRC = ("z", "xl")
SWAP = [(0, 1), (1, 0)]


def decode(codes_ref, scale_ref, step, tile):
    blocks = tile // EXP_BLOCK
    scale = pltpu.roll(scale_ref[...], 128 - blocks * step, 1)
    parts = []
    for b in range(blocks):
        wide = jnp.broadcast_to(scale[:, b : b + 1], (scale.shape[0], EXP_BLOCK)).astype(jnp.bfloat16)
        cols = slice(b * EXP_BLOCK, (b + 1) * EXP_BLOCK)
        parts.append(jnp.concatenate([codes_ref[0, :, cols] * wide, codes_ref[1, :, cols] * wide], axis=0))
    return jnp.concatenate(parts, axis=1)


def forward_body(tile, rows, mine_ref, other_ref, codes_ref, scale_ref, out_ref, acc_ref):
    step = pl.program_id(0)

    @pl.when(step == 0)
    def _():
        acc_ref[...] = jnp.zeros_like(acc_ref)

    kern = decode(codes_ref, scale_ref, step, tile)
    waves = jnp.concatenate([mine_ref[...], other_ref[...]], axis=0)
    acc_ref[...] += lax.dot_general(waves, kern, (((1,), (1,)), ((), ())), preferred_element_type=jnp.float32)

    @pl.when(step == pl.num_programs(0) - 1)
    def _():
        for c in range(2):
            for xy in range(8):
                at = c * 128 + xy * 16
                re, im = acc_ref[at : at + 8, :], acc_ref[at + 8 : at + 16, :]
                out_ref[xy, c, 0] = re[:, :rows] - im[:, rows:]
                out_ref[xy, c, 1] = im[:, :rows] + re[:, rows:]


def forward(mine, other, codes, scale, tile=1024):
    _, rows, cols = codes.shape
    import functools

    return pl.pallas_call(
        functools.partial(forward_body, tile, rows),
        grid=(cols // tile,),
        in_specs=[
            pl.BlockSpec((128, tile), lambda i: (0, i)),
            pl.BlockSpec((128, tile), lambda i: (0, i)),
            pl.BlockSpec((2, rows, tile), lambda i: (0, 0, i)),
            pl.BlockSpec((rows, 128), lambda i: (0, 0)),
        ],
        out_specs=pl.BlockSpec((8, 2, 2, 8, rows), lambda i: (0, 0, 0, 0, 0)),
        out_shape=jax.ShapeDtypeStruct((8, 2, 2, 8, rows), jnp.float32),
        scratch_shapes=[pltpu.VMEM((256, 2 * rows), jnp.float32)],
        cost_estimate=pl.CostEstimate(flops=2 * 256 * 1024 * 8192, bytes_accessed=22 << 20, transcendentals=0),
        name="forward",
    )(mine, other, codes, scale)


def backward_body(tile, amat_ref, codes_ref, scale_ref, mine_ref, other_ref):
    kern = decode(codes_ref, scale_ref, pl.program_id(0), tile)
    prod = jnp.dot(amat_ref[...], kern, preferred_element_type=jnp.float32).astype(jnp.bfloat16)
    mine_ref[...] = prod[:128]
    other_ref[...] = prod[128:]


def backward(amat, codes, scale, tile=1024):
    _, rows, cols = codes.shape
    import functools

    half = jax.ShapeDtypeStruct((128, cols), jnp.bfloat16)
    return pl.pallas_call(
        functools.partial(backward_body, tile),
        grid=(cols // tile,),
        in_specs=[
            pl.BlockSpec((256, 2 * rows), lambda i: (0, 0)),
            pl.BlockSpec((2, rows, tile), lambda i: (0, 0, i)),
            pl.BlockSpec((rows, 128), lambda i: (0, 0)),
        ],
        out_specs=[pl.BlockSpec((128, tile), lambda i: (0, i))] * 2,
        out_shape=[half, half],
        cost_estimate=pl.CostEstimate(flops=2 * 256 * 1024 * 8192, bytes_accessed=22 << 20, transcendentals=0),
        name="backward",
    )(amat, codes, scale)


def body(codes, exps, wavefield, observed, mask):
    _, rows, cols = codes.shape
    core = lax.axis_index("c")
    scale = jnp.exp2(exps.astype(jnp.float32))
    scale = jnp.concatenate([scale, scale], axis=1)
    own = wavefield.transpose(0, 2, 1)
    mine = lax.all_to_all(jnp.broadcast_to(own[None], (8,) + own.shape), XY, 0, 0, tiled=True)
    other = lax.ppermute(mine, "c", SWAP)
    parts = forward(mine.reshape(128, cols), other.reshape(128, cols), codes, scale)
    parts = lax.all_to_all(parts, SRC, 0, 0, tiled=True)
    pred = jnp.sum(parts, axis=0)
    share = lax.axis_index(SRC) * 16
    seen = lax.dynamic_slice_in_dim(observed, share, 16, 2)
    seen = seen.astype(jnp.float32).transpose(0, 2, 1).reshape(2, 2, 8, rows).transpose(1, 0, 2, 3)
    seen = jnp.where(core == 0, seen, seen[::-1])
    live = mask.astype(jnp.float32)
    resid = (live * (pred - seen)).astype(jnp.bfloat16)
    placed = jnp.where(core == 0, resid, resid[::-1])
    own_resid = placed.transpose(1, 0, 2, 3).reshape(2, 16, rows).transpose(0, 2, 1)
    every = lax.all_to_all(jnp.broadcast_to(resid[None], (8,) + resid.shape), SRC, 0, 0, tiled=True)
    every = every.transpose(1, 0, 2, 3, 4)
    re, im = every[:, :, 0], every[:, :, 1]
    amat = jnp.stack([jnp.concatenate([re, im], axis=3), jnp.concatenate([im, -re], axis=3)], axis=2)
    gmine, gother = backward(amat.reshape(256, 2 * rows), codes, scale)
    came = lax.ppermute(gother, "c", SWAP)
    chip = (gmine.astype(jnp.float32) + came.astype(jnp.float32)).astype(jnp.bfloat16)
    terms = lax.all_to_all(chip.reshape(8, 2, 8, cols), XY, 0, 0, tiled=True)
    gradient = jnp.sum(terms.astype(jnp.float32), axis=0).astype(jnp.bfloat16)
    return own_resid, gradient.transpose(0, 2, 1)


def solution(mesh):
    fine = Mesh(mesh.devices.reshape(2, 4, 2, 4, 2), ("xh", "y", "c", "z", "xl"))
    in_specs = (P(None, RCV, SRC), P(RCV, SRC), P(None, SRC, RCV), P(None, RCV, None), P(RCV))
    out_specs = (P(None, RCV, SRC), P(None, SRC, RCV))
    return jax.shard_map(body, mesh=fine, in_specs=in_specs, out_specs=out_specs, check_vma=False)
```

```python
import functools

import jax
import jax.numpy as jnp
from jax import lax
from jax.experimental import pallas as pl
from jax.experimental.pallas import tpu as pltpu
from jax.sharding import Mesh, PartitionSpec as P

EXP_BLOCK = 128
RCV = ("xh", "y", "c")
SRC = ("z", "xl")
SWAP = [(0, 1), (1, 0)]
VM = pl.BlockSpec(memory_space=pltpu.VMEM)

X, Y1, Y3, Y2 = (1, 0), (0, 1), (0, 3), (0, 2)
FROM = (
    ((0, 0), (1, 0), (0, 3), (0, 1), (0, 2), (1, 3), (1, 1), (1, 2)),
    ((0, 0), (0, 3), (0, 1), (0, 2), (1, 0), (1, 3), (1, 1), (1, 2)),
)
DEST = (
    ((0, 1), (1, 1), (0, 3), (1, 3), (0, 2), (1, 2), (0, 0), (1, 0)),
    ((1, 0), (1, 1), (1, 3), (1, 2), (0, 0), (0, 1), (0, 3), (0, 2)),
)


def move(x, first, second):
    pairs = []
    for a in range(2):
        for b in range(4):
            for c, step in ((0, first), (1, second)):
                if step is not None:
                    to = ((a + step[0]) % 2) * 4 + (b + step[1]) % 4
                    pairs.append(((a * 4 + b) * 2 + c, to * 2 + c))
    return lax.ppermute(x, RCV, pairs)


def swap(x):
    return lax.ppermute(x, "c", SWAP)


def vmem(x):
    return pltpu.with_memory_space_constraint(x, pltpu.VMEM)


def params(mib):
    return pltpu.CompilerParams(vmem_limit_bytes=mib << 20)


def cost(us):
    return pl.CostEstimate(flops=us * 10**9, bytes_accessed=us * 3 * 10**6, transcendentals=0)


def here(core, table, k):
    x, y = lax.axis_index("xh"), lax.axis_index("y")
    (ax, ay), (bx, by) = table[0][k], table[1][k]
    dx, dy = jnp.where(core == 0, ax, bx), jnp.where(core == 0, ay, by)
    return lax.bitwise_and(x + dx, 1) * 4 + lax.bitwise_and(y + dy, 3)


def decode(codes_ref, wide_ref, cols):
    wide = wide_ref[:, cols]
    return jnp.concatenate([codes_ref[0, :, cols] * wide, codes_ref[1, :, cols] * wide], axis=0)


def widen_body(exps_ref, wide_ref):
    exps = exps_ref[...]
    scale = jnp.where(exps >= -14, 2.0**-14, jnp.where(exps == -15, 2.0**-15, jnp.where(exps == -16, 2.0**-16, 2.0**-17)))
    scale = scale.astype(jnp.float32).T
    for b in range(exps.shape[0]):
        wide = jnp.broadcast_to(scale[:, b : b + 1], (scale.shape[0], EXP_BLOCK)).astype(jnp.bfloat16)
        wide_ref[:, b * EXP_BLOCK : (b + 1) * EXP_BLOCK] = wide


def widen(exps):
    blocks, rows = exps.shape
    return pl.pallas_call(
        widen_body,
        in_specs=[VM],
        out_specs=VM,
        out_shape=pltpu.VMEM((rows, blocks * EXP_BLOCK), jnp.bfloat16),
        cost_estimate=cost(10),
        compiler_params=params(4),
        name="widen",
    )(exps)


def pick_body(first, second, out):
    core = lax.axis_index("c")

    @pl.when(core == 0)
    def _():
        out[...] = first[...]

    @pl.when(core == 1)
    def _():
        out[...] = second[...]


def pick(first, second):
    return pl.pallas_call(
        pick_body,
        in_specs=[VM] * 2,
        out_specs=VM,
        out_shape=jax.ShapeDtypeStruct(first.shape, first.dtype),
        cost_estimate=cost(1),
        compiler_params=params(4),
        name="pick",
    )(first, second)


def forward_body(tile, rows, *refs):
    pieces, codes_ref, wide_ref, out_ref, acc_ref = refs[:16], refs[16], refs[17], refs[18], refs[19]
    acc_ref[...] = jnp.zeros_like(acc_ref)

    def step(i, _):
        at = pl.multiple_of(i * tile, tile)
        waves = jnp.concatenate([p[:, pl.ds(at, tile)] for p in pieces], axis=0)
        kern = decode(codes_ref, wide_ref, pl.ds(at, tile))
        acc_ref[...] += lax.dot_general(waves, kern, (((1,), (1,)), ((), ())), preferred_element_type=jnp.float32)
        return 0

    lax.fori_loop(0, pieces[0].shape[1] // tile, step, 0)
    core = lax.axis_index("c")
    for c in range(2):
        for k in range(8):
            at, top = here(lax.bitwise_xor(core, c), FROM, k), (c * 8 + k) * 16
            re, im = acc_ref[top : top + 8, :], acc_ref[top + 8 : top + 16, :]
            out_ref[at, c, 0] = re[:, :rows] - im[:, rows:]
            out_ref[at, c, 1] = im[:, :rows] + re[:, rows:]


def forward(pieces, codes, wide, tile=1024):
    rows = codes.shape[1]
    return pl.pallas_call(
        functools.partial(forward_body, tile, rows),
        in_specs=[VM] * 18,
        out_specs=VM,
        out_shape=jax.ShapeDtypeStruct((8, 2, 2, 8, rows), jnp.float32),
        scratch_shapes=[pltpu.VMEM((256, 2 * rows), jnp.float32)],
        cost_estimate=cost(6),
        compiler_params=params(10),
        name="forward",
    )(*pieces, vmem(codes), vmem(wide))


def resid_body(parts, seen, mask, every, own):
    core = lax.axis_index("c")
    live = mask[...].astype(jnp.float32)
    for c in range(2):
        at = lax.bitwise_xor(core, c)
        for k in range(2):
            pred = parts[0, c, k]
            for j in range(1, 8):
                pred += parts[j, c, k]
            resid = (live * (pred - seen[k, at])).astype(jnp.bfloat16)
            own[k, at] = resid
            for j in range(8):
                every[j, c, k] = resid


def residual(parts, seen, mask):
    one = jax.ShapeDtypeStruct(seen.shape, jnp.bfloat16)
    return pl.pallas_call(
        resid_body,
        in_specs=[VM] * 3,
        out_specs=[VM] * 2,
        out_shape=[jax.ShapeDtypeStruct(parts.shape, jnp.bfloat16), one],
        cost_estimate=cost(1),
        compiler_params=params(4),
        name="residual",
    )(parts, seen, mask)


def backward_body(start, tile, every_ref, codes_ref, wide_ref, *refs):
    other_ref, mine, a_ref = refs[0], refs[1:5], refs[5]
    rows = codes_ref.shape[1]
    core = lax.axis_index("c")
    for k in range(16):
        block = every_ref[here(lax.bitwise_xor(core, k // 8), DEST, k % 8), k // 8].astype(jnp.float32)
        top = slice(16 * k, 16 * k + 16)
        a_ref[top, :rows] = jnp.concatenate([block[0], block[1]], axis=0).astype(jnp.bfloat16)
        a_ref[top, rows:] = jnp.concatenate([block[1], -block[0]], axis=0).astype(jnp.bfloat16)

    def step(i, _):
        at = pl.multiple_of(start + i * tile, tile)
        to = pl.ds(pl.multiple_of(i * tile, tile), tile)
        kern = decode(codes_ref, wide_ref, pl.ds(at, tile))
        prod = jnp.dot(a_ref[...], kern, preferred_element_type=jnp.float32).astype(jnp.bfloat16)
        for k in range(8):
            mine[k // 2][k % 2, :, to] = prod[16 * k : 16 * k + 16]
            other_ref[k, :, to] = prod[128 + 16 * k : 144 + 16 * k]
        return 0

    lax.fori_loop(0, other_ref.shape[2] // tile, step, 0)


def backward(every, codes, wide, part, parts, tile=1024):
    _, rows, cols = codes.shape
    cols = cols // parts
    pair = jax.ShapeDtypeStruct((2, 16, cols), jnp.bfloat16)
    return pl.pallas_call(
        functools.partial(backward_body, part * cols, tile),
        in_specs=[VM] * 3,
        out_specs=[VM] * 5,
        out_shape=[jax.ShapeDtypeStruct((8, 16, cols), jnp.bfloat16)] + [pair] * 4,
        scratch_shapes=[pltpu.VMEM((256, 2 * rows), jnp.bfloat16)],
        cost_estimate=cost(3),
        compiler_params=params(10),
        name="backward",
    )(every, vmem(codes), vmem(wide))


def chip_body(m1, m2, m3, m4, came, u1, u2, u3, u4):
    for k, (m, u) in enumerate(((m1, u1), (m2, u2), (m3, u3), (m4, u4))):
        total = m[...].astype(jnp.float32) + came[2 * k : 2 * k + 2].astype(jnp.float32)
        u[...] = total.astype(jnp.bfloat16)


def chip_sum(mine, came):
    return pl.pallas_call(
        chip_body,
        in_specs=[VM] * 5,
        out_specs=[VM] * 4,
        out_shape=[jax.ShapeDtypeStruct(m.shape, m.dtype) for m in mine],
        cost_estimate=cost(1),
        compiler_params=params(4),
        name="chip_sum",
    )(*mine, came)


def stage_body(u3, u4, q1, q2, q3, keep, s4, s5, s6):
    def f(ref, k):
        return ref[k].astype(jnp.float32)

    core = lax.axis_index("c")

    @pl.when(core == 0)
    def _():
        keep[...] = f(u4, 0) + f(q1, 0) + f(q2, 0) + f(q3, 0)
        s4[...] = (f(u4, 1) + f(q1, 1) + f(q2, 1) + f(q3, 1)).astype(jnp.bfloat16)
        s5[...] = jnp.zeros_like(s5)
        s6[...] = jnp.zeros_like(s6)

    @pl.when(core == 1)
    def _():
        keep[...] = f(u3, 0) + f(q1, 0)
        s4[...] = (f(u3, 1) + f(q1, 1)).astype(jnp.bfloat16)
        s5[...] = (f(u4, 0) + f(q2, 0)).astype(jnp.bfloat16)
        s6[...] = (f(u4, 1) + f(q2, 1)).astype(jnp.bfloat16)


def stage_sum(u3, u4, q1, q2, q3):
    one = jax.ShapeDtypeStruct(u3.shape[1:], jnp.bfloat16)
    return pl.pallas_call(
        stage_body,
        in_specs=[VM] * 5,
        out_specs=[VM] * 4,
        out_shape=[jax.ShapeDtypeStruct(u3.shape[1:], jnp.float32), one, one, one],
        cost_estimate=cost(1),
        compiler_params=params(4),
        name="stage_sum",
    )(u3, u4, q1, q2, q3)


def gather(own, ready):
    r1 = move(own, X, Y1)
    r2 = move(own, Y1, Y3)
    r3 = move(own, Y3, Y2)
    r4 = move(own, Y2, X)
    r1, ready = lax.optimization_barrier((r1, ready))
    r5 = move(r1, Y1, X)
    r6 = move(pick(r1, r2), Y3, X)
    r7 = move(pick(r1, r3), Y2, X)
    return [own, r1, r2, r3, r4, r5, r6, r7], ready


def scatter(mine, came):
    u1, u2, u3, u4 = chip_sum(mine, came)
    q1 = move(u1, Y1, X)
    q2 = move(u2, Y3, X)
    q3 = move(u3, Y2, None)
    keep, s4, s5, s6 = stage_sum(u3, u4, q1, q2, q3)
    q4 = move(s4, X, Y1)
    q5 = move(s5, None, Y3)
    q6 = move(s6, None, Y2)
    return keep + q4.astype(jnp.float32) + q5.astype(jnp.float32) + q6.astype(jnp.float32)


def body(codes, exps, wavefield, observed, mask):
    _, rows, cols = codes.shape
    own = wavefield.transpose(0, 2, 1).reshape(16, cols)
    seen = lax.dynamic_slice_in_dim(observed, lax.axis_index(SRC) * 16, 16, 2)
    seen = seen.astype(jnp.float32).transpose(0, 2, 1).reshape(2, 2, 8, rows)
    pieces, (exps, seen, mask) = gather(own, (exps.T, seen, mask.reshape(1, rows)))
    wide = widen(exps)
    pieces += [swap(p) for p in pieces]
    parts = forward(pieces, codes, wide)
    parts = lax.all_to_all(parts, SRC, 0, 0, tiled=True)
    every, own_resid = residual(parts, seen, mask)
    every = lax.all_to_all(every, SRC, 0, 0, tiled=True)
    halves = []
    for part in range(2):
        other, *mine = backward(every, codes, wide, part, 2)
        halves.append((mine, swap(other)))
    sums = [scatter(mine, came) for mine, came in halves]
    gradient = jnp.concatenate(sums, axis=1).astype(jnp.bfloat16).reshape(2, 8, cols)
    return own_resid.reshape(2, 16, rows).transpose(0, 2, 1), gradient.transpose(0, 2, 1)


def solution(mesh):
    fine = Mesh(mesh.devices.reshape(2, 4, 2, 4, 2), ("xh", "y", "c", "z", "xl"))
    in_specs = (P(None, RCV, SRC), P(RCV, SRC), P(None, SRC, RCV), P(None, RCV, None), P(RCV))
    out_specs = (P(None, RCV, SRC), P(None, SRC, RCV))
    return jax.shard_map(body, mesh=fine, in_specs=in_specs, out_specs=out_specs, check_vma=False)
```

```python
import functools

import jax
import jax.numpy as jnp
from jax import lax
from jax.experimental import pallas as pl
from jax.experimental.pallas import tpu as pltpu
from jax.sharding import Mesh, PartitionSpec as P

EXP_BLOCK = 128
RCV = ("xh", "y", "c")
SRC = ("z", "xl")
SWAP = [(0, 1), (1, 0)]
VM = pl.BlockSpec(memory_space=pltpu.VMEM)

X, Y1, Y3, Y2 = (1, 0), (0, 1), (0, 3), (0, 2)
FROM = (
    ((0, 0), (1, 0), (0, 3), (0, 1), (0, 2), (1, 3), (1, 1), (1, 2)),
    ((0, 0), (0, 3), (0, 1), (0, 2), (1, 0), (1, 3), (1, 1), (1, 2)),
)
DEST = (
    ((0, 1), (1, 1), (0, 3), (1, 3), (0, 2), (1, 2), (0, 0), (1, 0)),
    ((1, 0), (1, 1), (1, 3), (1, 2), (0, 0), (0, 1), (0, 3), (0, 2)),
)


def move(x, first, second):
    pairs = []
    for a in range(2):
        for b in range(4):
            for c, step in ((0, first), (1, second)):
                if step is not None:
                    to = ((a + step[0]) % 2) * 4 + (b + step[1]) % 4
                    pairs.append(((a * 4 + b) * 2 + c, to * 2 + c))
    return lax.ppermute(x, RCV, pairs)


def swap(x):
    return lax.ppermute(x, "c", SWAP)


def vmem(x):
    return pltpu.with_memory_space_constraint(x, pltpu.VMEM)


def params(mib):
    return pltpu.CompilerParams(vmem_limit_bytes=mib << 20)


def cost(us):
    return pl.CostEstimate(flops=us * 10**9, bytes_accessed=us * 3 * 10**6, transcendentals=0)


def here(core, table, k):
    x, y = lax.axis_index("xh"), lax.axis_index("y")
    (ax, ay), (bx, by) = table[0][k], table[1][k]
    dx, dy = jnp.where(core == 0, ax, bx), jnp.where(core == 0, ay, by)
    return lax.bitwise_and(x + dx, 1) * 4 + lax.bitwise_and(y + dy, 3)


def decode(codes_ref, wide_ref, cols):
    wide = wide_ref[:, cols]
    return jnp.concatenate([codes_ref[0, :, cols] * wide, codes_ref[1, :, cols] * wide], axis=0)


def prepare_body(exps_ref, observed_ref, wide_ref, seen_ref, turn_ref):
    exps = exps_ref[...]
    scale = jnp.where(exps >= -14, 2.0**-14, jnp.where(exps == -15, 2.0**-15, jnp.where(exps == -16, 2.0**-16, 2.0**-17)))
    scale = scale.astype(jnp.float32).T
    for b in range(exps.shape[0]):
        wide = jnp.broadcast_to(scale[:, b : b + 1], (scale.shape[0], EXP_BLOCK)).astype(jnp.bfloat16)
        wide_ref[:, b * EXP_BLOCK : (b + 1) * EXP_BLOCK] = wide
    share = lax.axis_index("z") * 2 + lax.axis_index("xl")
    for k in range(2):
        turn_ref[...] = observed_ref[k].astype(jnp.float32).T
        for c in range(2):
            seen_ref[k, c] = turn_ref[pl.ds(pl.multiple_of(share * 16 + c * 8, 8), 8), :]


def prepare(exps, observed):
    blocks, rows = exps.shape
    return pl.pallas_call(
        prepare_body,
        in_specs=[VM] * 2,
        out_specs=[VM] * 2,
        out_shape=[pltpu.VMEM((rows, blocks * EXP_BLOCK), jnp.bfloat16), pltpu.VMEM((2, 2, 8, rows), jnp.float32)],
        scratch_shapes=[pltpu.VMEM((observed.shape[2], rows), jnp.float32)],
        cost_estimate=cost(4),
        compiler_params=params(6),
        name="prepare",
    )(exps, observed)


def pick_body(first, second, out):
    core = lax.axis_index("c")

    @pl.when(core == 0)
    def _():
        out[...] = first[...]

    @pl.when(core == 1)
    def _():
        out[...] = second[...]


def pick(first, second):
    return pl.pallas_call(
        pick_body,
        in_specs=[VM] * 2,
        out_specs=VM,
        out_shape=jax.ShapeDtypeStruct(first.shape, first.dtype),
        cost_estimate=cost(8),
        compiler_params=params(4),
        name="pick",
    )(first, second)


def forward_body(tile, rows, *refs):
    pieces, codes_ref, wide_ref, out_ref, acc_ref = refs[:16], refs[16], refs[17], refs[18], refs[19]
    acc_ref[...] = jnp.zeros_like(acc_ref)

    def step(i, _):
        at = pl.multiple_of(i * tile, tile)
        waves = jnp.concatenate([p[:, pl.ds(at, tile)] for p in pieces], axis=0)
        kern = decode(codes_ref, wide_ref, pl.ds(at, tile))
        acc_ref[...] += lax.dot_general(waves, kern, (((1,), (1,)), ((), ())), preferred_element_type=jnp.float32)
        return 0

    lax.fori_loop(0, pieces[0].shape[1] // tile, step, 0)
    core = lax.axis_index("c")
    for c in range(2):
        for k in range(8):
            at, top = here(lax.bitwise_xor(core, c), FROM, k), (c * 8 + k) * 16
            re, im = acc_ref[top : top + 8, :], acc_ref[top + 8 : top + 16, :]
            out_ref[at, c, 0] = re[:, :rows] - im[:, rows:]
            out_ref[at, c, 1] = im[:, :rows] + re[:, rows:]


def forward(pieces, codes, wide, tile=8192):
    rows = codes.shape[1]
    return pl.pallas_call(
        functools.partial(forward_body, tile, rows),
        in_specs=[VM] * 18,
        out_specs=VM,
        out_shape=jax.ShapeDtypeStruct((8, 2, 2, 8, rows), jnp.float32),
        scratch_shapes=[pltpu.VMEM((256, 2 * rows), jnp.float32)],
        cost_estimate=cost(6),
        compiler_params=params(10),
        name="forward",
    )(*pieces, vmem(codes), vmem(wide))


def resid_body(parts, seen, mask, every, own):
    core = lax.axis_index("c")
    live = mask[...].astype(jnp.float32)
    for c in range(2):
        at = lax.bitwise_xor(core, c)
        for k in range(2):
            pred = parts[0, c, k]
            for j in range(1, 8):
                pred += parts[j, c, k]
            resid = (live * (pred - seen[k, at])).astype(jnp.bfloat16)
            own[k, at] = resid
            for j in range(8):
                every[j, c, k] = resid


def residual(parts, seen, mask):
    one = jax.ShapeDtypeStruct(seen.shape, jnp.bfloat16)
    return pl.pallas_call(
        resid_body,
        in_specs=[VM] * 3,
        out_specs=[VM] * 2,
        out_shape=[jax.ShapeDtypeStruct(parts.shape, jnp.bfloat16), one],
        cost_estimate=cost(1),
        compiler_params=params(4),
        name="residual",
    )(parts, seen, mask)


def backward_body(which, tile, every_ref, codes_ref, wide_ref, *refs):
    outs, a_ref = refs[:-1], refs[-1]
    rows = codes_ref.shape[1]
    owner = lax.bitwise_xor(lax.axis_index("c"), which)
    for k in range(8):
        block = every_ref[here(owner, DEST, k), which].astype(jnp.float32)
        top = slice(16 * k, 16 * k + 16)
        a_ref[top, :rows] = jnp.concatenate([block[0], block[1]], axis=0).astype(jnp.bfloat16)
        a_ref[top, rows:] = jnp.concatenate([block[1], -block[0]], axis=0).astype(jnp.bfloat16)

    def step(i, _):
        cols = pl.ds(pl.multiple_of(i * tile, tile), tile)
        kern = decode(codes_ref, wide_ref, cols)
        prod = jnp.dot(a_ref[...], kern, preferred_element_type=jnp.float32).astype(jnp.bfloat16)
        each = 8 // len(outs)
        for k in range(8):
            outs[k // each][k % each, :, cols] = prod[16 * k : 16 * k + 16]
        return 0

    lax.fori_loop(0, codes_ref.shape[2] // tile, step, 0)


def backward(every, codes, wide, which, count, tile=8192):
    _, rows, cols = codes.shape
    return pl.pallas_call(
        functools.partial(backward_body, which, tile),
        in_specs=[VM] * 3,
        out_specs=[VM] * count,
        out_shape=[jax.ShapeDtypeStruct((8 // count, 16, cols), jnp.bfloat16)] * count,
        scratch_shapes=[pltpu.VMEM((128, 2 * rows), jnp.bfloat16)],
        cost_estimate=cost(3),
        compiler_params=params(8),
        name="backward",
    )(every, vmem(codes), vmem(wide))


def chip_body(m1, m2, m3, m4, came, u1, u2, u3, u4):
    for k, (m, u) in enumerate(((m1, u1), (m2, u2), (m3, u3), (m4, u4))):
        total = m[...].astype(jnp.float32) + came[2 * k : 2 * k + 2].astype(jnp.float32)
        u[...] = total.astype(jnp.bfloat16)


def chip_sum(mine, came):
    return pl.pallas_call(
        chip_body,
        in_specs=[VM] * 5,
        out_specs=[VM] * 4,
        out_shape=[jax.ShapeDtypeStruct(m.shape, m.dtype) for m in mine],
        cost_estimate=cost(1),
        compiler_params=params(4),
        name="chip_sum",
    )(*mine, came)


def stage_body(u3, u4, q1, q2, q3, keep, s4, s5, s6):
    def f(ref, k):
        return ref[k].astype(jnp.float32)

    core = lax.axis_index("c")

    @pl.when(core == 0)
    def _():
        keep[...] = f(u4, 0) + f(q1, 0) + f(q2, 0) + f(q3, 0)
        s4[...] = (f(u4, 1) + f(q1, 1) + f(q2, 1) + f(q3, 1)).astype(jnp.bfloat16)
        s5[...] = jnp.zeros_like(s5)
        s6[...] = jnp.zeros_like(s6)

    @pl.when(core == 1)
    def _():
        keep[...] = f(u3, 0) + f(q1, 0)
        s4[...] = (f(u3, 1) + f(q1, 1)).astype(jnp.bfloat16)
        s5[...] = (f(u4, 0) + f(q2, 0)).astype(jnp.bfloat16)
        s6[...] = (f(u4, 1) + f(q2, 1)).astype(jnp.bfloat16)


def stage_sum(u3, u4, q1, q2, q3):
    one = jax.ShapeDtypeStruct(u3.shape[1:], jnp.bfloat16)
    return pl.pallas_call(
        stage_body,
        in_specs=[VM] * 5,
        out_specs=[VM] * 4,
        out_shape=[jax.ShapeDtypeStruct(u3.shape[1:], jnp.float32), one, one, one],
        cost_estimate=cost(1),
        compiler_params=params(4),
        name="stage_sum",
    )(u3, u4, q1, q2, q3)


def gather(own):
    r1 = move(own, X, Y1)
    r2 = move(own, Y1, Y3)
    r3 = move(own, Y3, Y2)
    r4 = move(own, Y2, X)
    r5 = move(r1, Y1, X)
    r6 = move(pick(r1, r2), Y3, X)
    r7 = move(pick(r1, r3), Y2, X)
    return [own, r1, r2, r3, r4, r5, r6, r7]


def scatter(mine, came):
    u1, u2, u3, u4 = chip_sum(mine, came)
    q1 = move(u1, Y1, X)
    q2 = move(u2, Y3, X)
    q3 = move(u3, Y2, None)
    keep, s4, s5, s6 = stage_sum(u3, u4, q1, q2, q3)
    q4 = move(s4, X, Y1)
    q5 = move(s5, None, Y3)
    q6 = move(s6, None, Y2)
    return keep + q4.astype(jnp.float32) + q5.astype(jnp.float32) + q6.astype(jnp.float32)


def body(codes, exps, wavefield, observed, mask):
    _, rows, cols = codes.shape
    own = wavefield.transpose(0, 2, 1).reshape(16, cols)
    pieces = gather(own)
    wide, seen = prepare(exps.T, observed)
    pieces += [swap(p) for p in pieces]
    parts = forward(pieces, codes, wide)
    parts = lax.all_to_all(parts, SRC, 0, 0, tiled=True)
    every, own_resid = residual(parts, vmem(seen), mask.reshape(1, rows))
    every = lax.all_to_all(every, SRC, 0, 0, tiled=True)
    (other,) = backward(every, codes, wide, 1, 1)
    came = swap(other)
    mine = backward(every, codes, wide, 0, 4)
    gradient = scatter(mine, came)
    gradient = gradient.astype(jnp.bfloat16).reshape(2, 8, cols)
    return own_resid.reshape(2, 16, rows).transpose(0, 2, 1), gradient.transpose(0, 2, 1)


def solution(mesh):
    fine = Mesh(mesh.devices.reshape(2, 4, 2, 4, 2), ("xh", "y", "c", "z", "xl"))
    in_specs = (P(None, RCV, SRC), P(RCV, SRC), P(None, SRC, RCV), P(None, RCV, None), P(RCV))
    out_specs = (P(None, RCV, SRC), P(None, SRC, RCV))
    return jax.shard_map(body, mesh=fine, in_specs=in_specs, out_specs=out_specs, check_vma=False)
```

```python
import functools

import jax
import jax.numpy as jnp
from jax import lax
from jax.experimental import pallas as pl
from jax.experimental.pallas import tpu as pltpu
from jax.sharding import Mesh, PartitionSpec as P

EXP_BLOCK = 128
RCV = ("xh", "y", "c")
SRC = ("z", "xl")
SWAP = [(0, 1), (1, 0)]
VM = pl.BlockSpec(memory_space=pltpu.VMEM)

X, Y1, Y3, Y2 = (1, 0), (0, 1), (0, 3), (0, 2)
FROM = (
    ((0, 0), (1, 0), (0, 3), (0, 1), (0, 2), (1, 3), (1, 1), (1, 2)),
    ((0, 0), (0, 3), (0, 1), (0, 2), (1, 0), (1, 3), (1, 1), (1, 2)),
)
DEST = (
    ((0, 1), (1, 1), (0, 3), (1, 3), (0, 2), (1, 2), (0, 0), (1, 0)),
    ((1, 0), (1, 1), (1, 3), (1, 2), (0, 0), (0, 1), (0, 3), (0, 2)),
)


def move(x, first, second):
    pairs = []
    for a in range(2):
        for b in range(4):
            for c, step in ((0, first), (1, second)):
                if step is not None:
                    to = ((a + step[0]) % 2) * 4 + (b + step[1]) % 4
                    pairs.append(((a * 4 + b) * 2 + c, to * 2 + c))
    return lax.ppermute(x, RCV, pairs)


def swap(x):
    return lax.ppermute(x, "c", SWAP)


def vmem(x):
    return pltpu.with_memory_space_constraint(x, pltpu.VMEM)


def params(mib):
    return pltpu.CompilerParams(vmem_limit_bytes=mib << 20)


def cost(us):
    return pl.CostEstimate(flops=us * 10**9, bytes_accessed=us * 3 * 10**6, transcendentals=0)


def here(core, table, k):
    x, y = lax.axis_index("xh"), lax.axis_index("y")
    (ax, ay), (bx, by) = table[0][k], table[1][k]
    dx, dy = jnp.where(core == 0, ax, bx), jnp.where(core == 0, ay, by)
    return lax.bitwise_and(x + dx, 1) * 4 + lax.bitwise_and(y + dy, 3)


def decode(codes_ref, wide_ref, cols):
    wide = wide_ref[:, cols]
    return jnp.concatenate([codes_ref[0, :, cols] * wide, codes_ref[1, :, cols] * wide], axis=0)


def prepare_body(exps_ref, observed_ref, wide_ref, seen_ref, turn_ref):
    exps = exps_ref[...]
    scale = jnp.where(exps >= -14, 2.0**-14, jnp.where(exps == -15, 2.0**-15, jnp.where(exps == -16, 2.0**-16, 2.0**-17)))
    scale = scale.astype(jnp.float32).T
    for b in range(exps.shape[0]):
        wide = jnp.broadcast_to(scale[:, b : b + 1], (scale.shape[0], EXP_BLOCK)).astype(jnp.bfloat16)
        wide_ref[:, b * EXP_BLOCK : (b + 1) * EXP_BLOCK] = wide
    share = lax.axis_index("z") * 2 + lax.axis_index("xl")
    for k in range(2):
        turn_ref[...] = observed_ref[k].astype(jnp.float32).T
        for c in range(2):
            seen_ref[k, c] = turn_ref[pl.ds(pl.multiple_of(share * 16 + c * 8, 8), 8), :]


def prepare(exps, observed):
    blocks, rows = exps.shape
    return pl.pallas_call(
        prepare_body,
        in_specs=[VM] * 2,
        out_specs=[VM] * 2,
        out_shape=[pltpu.VMEM((rows, blocks * EXP_BLOCK), jnp.bfloat16), pltpu.VMEM((2, 2, 8, rows), jnp.float32)],
        scratch_shapes=[pltpu.VMEM((observed.shape[2], rows), jnp.float32)],
        cost_estimate=cost(4),
        compiler_params=params(6),
        name="prepare",
    )(exps, observed)


def pick_body(first, second, out):
    core = lax.axis_index("c")

    @pl.when(core == 0)
    def _():
        out[...] = first[...]

    @pl.when(core == 1)
    def _():
        out[...] = second[...]


def pick(first, second):
    return pl.pallas_call(
        pick_body,
        in_specs=[VM] * 2,
        out_specs=VM,
        out_shape=jax.ShapeDtypeStruct(first.shape, first.dtype),
        cost_estimate=cost(8),
        compiler_params=params(4),
        name="pick",
    )(first, second)


def forward_body(tile, rows, *refs):
    pieces, codes_ref, wide_ref, out_ref, acc_ref = refs[:16], refs[16], refs[17], refs[18], refs[19]
    acc_ref[...] = jnp.zeros_like(acc_ref)

    def step(i, _):
        at = pl.multiple_of(i * tile, tile)
        waves = jnp.concatenate([p[:, pl.ds(at, tile)] for p in pieces], axis=0)
        kern = decode(codes_ref, wide_ref, pl.ds(at, tile))
        acc_ref[...] += lax.dot_general(waves, kern, (((1,), (1,)), ((), ())), preferred_element_type=jnp.float32)
        return 0

    lax.fori_loop(0, pieces[0].shape[1] // tile, step, 0)
    core = lax.axis_index("c")
    for c in range(2):
        for k in range(8):
            at, top = here(lax.bitwise_xor(core, c), FROM, k), (c * 8 + k) * 16
            re, im = acc_ref[top : top + 8, :], acc_ref[top + 8 : top + 16, :]
            out_ref[at, c, 0] = re[:, :rows] - im[:, rows:]
            out_ref[at, c, 1] = im[:, :rows] + re[:, rows:]


def forward(pieces, codes, wide, tile=8192):
    rows = codes.shape[1]
    return pl.pallas_call(
        functools.partial(forward_body, tile, rows),
        in_specs=[VM] * 18,
        out_specs=VM,
        out_shape=jax.ShapeDtypeStruct((8, 2, 2, 8, rows), jnp.float32),
        scratch_shapes=[pltpu.VMEM((256, 2 * rows), jnp.float32)],
        cost_estimate=cost(6),
        compiler_params=params(10),
        name="forward",
    )(*pieces, vmem(codes), vmem(wide))


def resid_body(parts, seen, mask, every, own):
    core = lax.axis_index("c")
    live = mask[...].astype(jnp.float32)
    for c in range(2):
        at = lax.bitwise_xor(core, c)
        for k in range(2):
            pred = parts[0, c, k]
            for j in range(1, 8):
                pred += parts[j, c, k]
            resid = (live * (pred - seen[k, at])).astype(jnp.bfloat16)
            own[k, at] = resid
            for j in range(8):
                every[j, c, k] = resid


def residual(parts, seen, mask):
    one = jax.ShapeDtypeStruct(seen.shape, jnp.bfloat16)
    return pl.pallas_call(
        resid_body,
        in_specs=[VM] * 3,
        out_specs=[VM] * 2,
        out_shape=[jax.ShapeDtypeStruct(parts.shape, jnp.bfloat16), one],
        cost_estimate=cost(1),
        compiler_params=params(4),
        name="residual",
    )(parts, seen, mask)


def backward_body(start, every_ref, codes_ref, wide_ref, other_ref, *refs):
    mine, a_ref = refs[:4], refs[4]
    rows = codes_ref.shape[1]
    core = lax.axis_index("c")
    for k in range(16):
        owner = lax.bitwise_xor(core, k // 8)
        block = every_ref[here(owner, DEST, k % 8), k // 8].astype(jnp.float32)
        top = slice(16 * k, 16 * k + 16)
        a_ref[top, :rows] = jnp.concatenate([block[0], block[1]], axis=0).astype(jnp.bfloat16)
        a_ref[top, rows:] = jnp.concatenate([block[1], -block[0]], axis=0).astype(jnp.bfloat16)
    kern = decode(codes_ref, wide_ref, slice(start, start + other_ref.shape[2]))
    prod = jnp.dot(a_ref[...], kern, preferred_element_type=jnp.float32).astype(jnp.bfloat16)
    for k in range(8):
        mine[k // 2][k % 2] = prod[16 * k : 16 * k + 16]
        other_ref[k] = prod[128 + 16 * k : 144 + 16 * k]


def backward(every, codes, wide, part, parts):
    _, rows, cols = codes.shape
    cols = cols // parts
    pair = jax.ShapeDtypeStruct((2, 16, cols), jnp.bfloat16)
    return pl.pallas_call(
        functools.partial(backward_body, part * cols),
        in_specs=[VM] * 3,
        out_specs=[VM] * 5,
        out_shape=[jax.ShapeDtypeStruct((8, 16, cols), jnp.bfloat16)] + [pair] * 4,
        scratch_shapes=[pltpu.VMEM((256, 2 * rows), jnp.bfloat16)],
        cost_estimate=cost(3),
        compiler_params=params(8),
        name="backward",
    )(every, vmem(codes), vmem(wide))


def chip_body(m1, m2, m3, m4, came, u1, u2, u3, u4):
    for k, (m, u) in enumerate(((m1, u1), (m2, u2), (m3, u3), (m4, u4))):
        total = m[...].astype(jnp.float32) + came[2 * k : 2 * k + 2].astype(jnp.float32)
        u[...] = total.astype(jnp.bfloat16)


def chip_sum(mine, came):
    return pl.pallas_call(
        chip_body,
        in_specs=[VM] * 5,
        out_specs=[VM] * 4,
        out_shape=[jax.ShapeDtypeStruct(m.shape, m.dtype) for m in mine],
        cost_estimate=cost(1),
        compiler_params=params(4),
        name="chip_sum",
    )(*mine, came)


def stage_body(parts, *refs):
    core = lax.axis_index("c")
    keep, s4, s5, s6 = refs[5 * parts :]
    cols = keep.shape[1] // parts

    def f(ref, k):
        return ref[k].astype(jnp.float32)

    for p in range(parts):
        u3, u4, q1, q2, q3 = refs[5 * p : 5 * p + 5]
        at = slice(p * cols, (p + 1) * cols)

        @pl.when(core == 0)
        def _():
            keep[:, at] = f(u4, 0) + f(q1, 0) + f(q2, 0) + f(q3, 0)
            s4[:, at] = (f(u4, 1) + f(q1, 1) + f(q2, 1) + f(q3, 1)).astype(jnp.bfloat16)

        @pl.when(core == 1)
        def _():
            keep[:, at] = f(u3, 0) + f(q1, 0)
            s4[:, at] = (f(u3, 1) + f(q1, 1)).astype(jnp.bfloat16)
            s5[:, at] = (f(u4, 0) + f(q2, 0)).astype(jnp.bfloat16)
            s6[:, at] = (f(u4, 1) + f(q2, 1)).astype(jnp.bfloat16)


def stage_sum(terms):
    parts = len(terms)
    _, rows, cols = terms[0][0].shape
    one = jax.ShapeDtypeStruct((rows, parts * cols), jnp.bfloat16)
    return pl.pallas_call(
        functools.partial(stage_body, parts),
        in_specs=[VM] * (5 * parts),
        out_specs=[VM] * 4,
        out_shape=[jax.ShapeDtypeStruct(one.shape, jnp.float32), one, one, one],
        cost_estimate=cost(1),
        compiler_params=params(4),
        name="stage_sum",
    )(*[x for t in terms for x in t])


def last_body(keep, q4, q5, q6, out):
    core = lax.axis_index("c")

    @pl.when(core == 0)
    def _():
        out[...] = (keep[...] + q4[...].astype(jnp.float32)).astype(jnp.bfloat16)

    @pl.when(core == 1)
    def _():
        total = keep[...] + q4[...].astype(jnp.float32)
        total += q5[...].astype(jnp.float32) + q6[...].astype(jnp.float32)
        out[...] = total.astype(jnp.bfloat16)


def last_sum(keep, q4, q5, q6):
    return pl.pallas_call(
        last_body,
        in_specs=[VM] * 4,
        out_specs=VM,
        out_shape=jax.ShapeDtypeStruct(q4.shape, q4.dtype),
        cost_estimate=cost(1),
        compiler_params=params(4),
        name="last_sum",
    )(keep, q4, q5, q6)


def gather(own):
    r1 = move(own, X, Y1)
    r2 = move(own, Y1, Y3)
    r3 = move(own, Y3, Y2)
    r4 = move(own, Y2, X)
    r5 = move(r1, Y1, X)
    r6 = move(pick(r1, r2), Y3, X)
    r7 = move(pick(r1, r3), Y2, X)
    return [own, r1, r2, r3, r4, r5, r6, r7]


def scatter(halves):
    terms = []
    for mine, came in halves:
        u1, u2, u3, u4 = chip_sum(mine, came)
        q1 = move(u1, Y1, X)
        q2 = move(u2, Y3, X)
        q3 = move(u3, Y2, None)
        terms.append((u3, u4, q1, q2, q3))
    keep, s4, s5, s6 = stage_sum(terms)
    q4 = move(s4, X, Y1)
    q5 = move(s5, None, Y3)
    q6 = move(s6, None, Y2)
    return last_sum(keep, q4, q5, q6)


def body(codes, exps, wavefield, observed, mask):
    _, rows, cols = codes.shape
    own = wavefield.transpose(0, 2, 1).reshape(16, cols)
    pieces = gather(own)
    wide, seen = prepare(exps.T, observed)
    pieces += [swap(p) for p in pieces]
    parts = forward(pieces, codes, wide)
    parts = lax.all_to_all(parts, SRC, 0, 0, tiled=True)
    every, own_resid = residual(parts, vmem(seen), mask.reshape(1, rows))
    every = lax.all_to_all(every, SRC, 0, 0, tiled=True)
    halves = []
    for p in range(2):
        other, *mine = backward(every, codes, wide, p, 2)
        halves.append((mine, swap(other)))
    gradient = scatter(halves)
    gradient = gradient.reshape(2, 8, cols)
    return own_resid.reshape(2, 16, rows).transpose(0, 2, 1), gradient.transpose(0, 2, 1)


def solution(mesh):
    fine = Mesh(mesh.devices.reshape(2, 4, 2, 4, 2), ("xh", "y", "c", "z", "xl"))
    in_specs = (P(None, RCV, SRC), P(RCV, SRC), P(None, SRC, RCV), P(None, RCV, None), P(RCV))
    out_specs = (P(None, RCV, SRC), P(None, SRC, RCV))
    return jax.shard_map(body, mesh=fine, in_specs=in_specs, out_specs=out_specs, check_vma=False)
```

```python
import functools

import jax
import jax.numpy as jnp
from jax import lax
from jax.experimental import pallas as pl
from jax.experimental.pallas import tpu as pltpu
from jax.sharding import Mesh, PartitionSpec as P

EXP_BLOCK = 128
RCV = ("xh", "y", "c")
SRC = ("z", "xl")
SWAP = [(0, 1), (1, 0)]
VM = pl.BlockSpec(memory_space=pltpu.VMEM)

X, Y1, Y3, Y2 = (1, 0), (0, 1), (0, 3), (0, 2)
FROM = (
    ((0, 0), (1, 0), (0, 3), (0, 1), (0, 2), (1, 3), (1, 1), (1, 2)),
    ((0, 0), (0, 3), (0, 2), (0, 1), (1, 0), (1, 3), (1, 2), (1, 1)),
)
DEST = (
    ((0, 1), (1, 1), (0, 3), (1, 3), (0, 2), (1, 2), (0, 0), (1, 0)),
    ((1, 0), (1, 1), (1, 3), (1, 2), (0, 0), (0, 1), (0, 3), (0, 2)),
)


def move(x, first, second):
    pairs = []
    for a in range(2):
        for b in range(4):
            for c, step in ((0, first), (1, second)):
                if step is not None:
                    to = ((a + step[0]) % 2) * 4 + (b + step[1]) % 4
                    pairs.append(((a * 4 + b) * 2 + c, to * 2 + c))
    return lax.ppermute(x, RCV, pairs)


def swap(x):
    return lax.ppermute(x, "c", SWAP)


def vmem(x):
    return pltpu.with_memory_space_constraint(x, pltpu.VMEM)


def params(mib):
    return pltpu.CompilerParams(vmem_limit_bytes=mib << 20)


def cost(us):
    return pl.CostEstimate(flops=us * 10**9, bytes_accessed=us * 3 * 10**6, transcendentals=0)


def here(core, table, k):
    x, y = lax.axis_index("xh"), lax.axis_index("y")
    (ax, ay), (bx, by) = table[0][k], table[1][k]
    dx, dy = jnp.where(core == 0, ax, bx), jnp.where(core == 0, ay, by)
    return lax.bitwise_and(x + dx, 1) * 4 + lax.bitwise_and(y + dy, 3)


def decode(codes_ref, wide_ref, cols):
    wide = wide_ref[:, cols]
    return jnp.concatenate([codes_ref[0, :, cols] * wide, codes_ref[1, :, cols] * wide], axis=0)


def prepare_body(exps_ref, observed_ref, wide_ref, seen_ref, turn_ref):
    exps = exps_ref[...]
    scale = jnp.where(exps >= -14, 2.0**-14, jnp.where(exps == -15, 2.0**-15, jnp.where(exps == -16, 2.0**-16, 2.0**-17)))
    scale = scale.astype(jnp.float32).T
    for b in range(exps.shape[0]):
        wide = jnp.broadcast_to(scale[:, b : b + 1], (scale.shape[0], EXP_BLOCK)).astype(jnp.bfloat16)
        wide_ref[:, b * EXP_BLOCK : (b + 1) * EXP_BLOCK] = wide
    share = lax.axis_index("z") * 2 + lax.axis_index("xl")
    for k in range(2):
        turn_ref[...] = observed_ref[k].astype(jnp.float32).T
        for c in range(2):
            seen_ref[k, c] = turn_ref[pl.ds(pl.multiple_of(share * 16 + c * 8, 8), 8), :]


def prepare(exps, observed):
    blocks, rows = exps.shape
    return pl.pallas_call(
        prepare_body,
        in_specs=[VM] * 2,
        out_specs=[VM] * 2,
        out_shape=[pltpu.VMEM((rows, blocks * EXP_BLOCK), jnp.bfloat16), pltpu.VMEM((2, 2, 8, rows), jnp.float32)],
        scratch_shapes=[pltpu.VMEM((observed.shape[2], rows), jnp.float32)],
        cost_estimate=cost(4),
        compiler_params=params(6),
        name="prepare",
    )(exps, observed)


def pick_body(first, second, out):
    core = lax.axis_index("c")

    @pl.when(core == 0)
    def _():
        out[...] = first[...]

    @pl.when(core == 1)
    def _():
        out[...] = second[...]


def pick(first, second):
    return pl.pallas_call(
        pick_body,
        in_specs=[VM] * 2,
        out_specs=VM,
        out_shape=jax.ShapeDtypeStruct(first.shape, first.dtype),
        cost_estimate=cost(8),
        compiler_params=params(4),
        name="pick",
    )(first, second)


def forward_body(tile, rows, *refs):
    pieces, codes_ref, wide_ref, out_ref, acc_ref = refs[:16], refs[16], refs[17], refs[18], refs[19]
    acc_ref[...] = jnp.zeros_like(acc_ref)

    def step(i, _):
        at = pl.multiple_of(i * tile, tile)
        waves = jnp.concatenate([p[:, pl.ds(at, tile)] for p in pieces], axis=0)
        kern = decode(codes_ref, wide_ref, pl.ds(at, tile))
        acc_ref[...] += lax.dot_general(waves, kern, (((1,), (1,)), ((), ())), preferred_element_type=jnp.float32)
        return 0

    lax.fori_loop(0, pieces[0].shape[1] // tile, step, 0)
    core = lax.axis_index("c")
    for c in range(2):
        for k in range(8):
            at, top = here(lax.bitwise_xor(core, c), FROM, k), (c * 8 + k) * 16
            re, im = acc_ref[top : top + 8, :], acc_ref[top + 8 : top + 16, :]
            out_ref[at, c, 0] = re[:, :rows] - im[:, rows:]
            out_ref[at, c, 1] = im[:, :rows] + re[:, rows:]


def forward(pieces, codes, wide, tile=8192):
    rows = codes.shape[1]
    return pl.pallas_call(
        functools.partial(forward_body, tile, rows),
        in_specs=[VM] * 18,
        out_specs=VM,
        out_shape=jax.ShapeDtypeStruct((8, 2, 2, 8, rows), jnp.float32),
        scratch_shapes=[pltpu.VMEM((256, 2 * rows), jnp.float32)],
        cost_estimate=cost(6),
        compiler_params=params(10),
        name="forward",
    )(*pieces, vmem(codes), vmem(wide))


def resid_body(parts, seen, mask, every, own):
    core = lax.axis_index("c")
    live = mask[...].astype(jnp.float32)
    for c in range(2):
        at = lax.bitwise_xor(core, c)
        for k in range(2):
            pred = parts[0, c, k]
            for j in range(1, 8):
                pred += parts[j, c, k]
            resid = (live * (pred - seen[k, at])).astype(jnp.bfloat16)
            own[k, at] = resid
            for j in range(8):
                every[j, c, k] = resid


def residual(parts, seen, mask):
    one = jax.ShapeDtypeStruct(seen.shape, jnp.bfloat16)
    return pl.pallas_call(
        resid_body,
        in_specs=[VM] * 3,
        out_specs=[VM] * 2,
        out_shape=[jax.ShapeDtypeStruct(parts.shape, jnp.bfloat16), one],
        cost_estimate=cost(1),
        compiler_params=params(4),
        name="residual",
    )(parts, seen, mask)


def backward_body(start, every_ref, codes_ref, wide_ref, other_ref, *refs):
    mine, a_ref = refs[:4], refs[4]
    rows = codes_ref.shape[1]
    core = lax.axis_index("c")
    for k in range(16):
        owner = lax.bitwise_xor(core, k // 8)
        block = every_ref[here(owner, DEST, k % 8), k // 8].astype(jnp.float32)
        top = slice(16 * k, 16 * k + 16)
        a_ref[top, :rows] = jnp.concatenate([block[0], block[1]], axis=0).astype(jnp.bfloat16)
        a_ref[top, rows:] = jnp.concatenate([block[1], -block[0]], axis=0).astype(jnp.bfloat16)
    kern = decode(codes_ref, wide_ref, slice(start, start + other_ref.shape[2]))
    prod = jnp.dot(a_ref[...], kern, preferred_element_type=jnp.float32).astype(jnp.bfloat16)
    for k in range(8):
        mine[k // 2][k % 2] = prod[16 * k : 16 * k + 16]
        other_ref[k] = prod[128 + 16 * k : 144 + 16 * k]


def backward(every, codes, wide, part, parts):
    _, rows, cols = codes.shape
    cols = cols // parts
    pair = jax.ShapeDtypeStruct((2, 16, cols), jnp.bfloat16)
    return pl.pallas_call(
        functools.partial(backward_body, part * cols),
        in_specs=[VM] * 3,
        out_specs=[VM] * 5,
        out_shape=[jax.ShapeDtypeStruct((8, 16, cols), jnp.bfloat16)] + [pair] * 4,
        scratch_shapes=[pltpu.VMEM((256, 2 * rows), jnp.bfloat16)],
        cost_estimate=cost(3),
        compiler_params=params(8),
        name="backward",
    )(every, vmem(codes), vmem(wide))


def chip_body(m1, m2, m3, m4, came, u1, u2, u3, u4):
    for k, (m, u) in enumerate(((m1, u1), (m2, u2), (m3, u3), (m4, u4))):
        total = m[...].astype(jnp.float32) + came[2 * k : 2 * k + 2].astype(jnp.float32)
        u[...] = total.astype(jnp.bfloat16)


def chip_sum(mine, came):
    return pl.pallas_call(
        chip_body,
        in_specs=[VM] * 5,
        out_specs=[VM] * 4,
        out_shape=[jax.ShapeDtypeStruct(m.shape, m.dtype) for m in mine],
        cost_estimate=cost(1),
        compiler_params=params(4),
        name="chip_sum",
    )(*mine, came)


def stage_body(parts, *refs):
    core = lax.axis_index("c")
    keep, s4, s5, s6 = refs[5 * parts :]
    cols = keep.shape[1] // parts

    def f(ref, k):
        return ref[k].astype(jnp.float32)

    for p in range(parts):
        u3, u4, q1, q2, q3 = refs[5 * p : 5 * p + 5]
        at = slice(p * cols, (p + 1) * cols)

        @pl.when(core == 0)
        def _():
            keep[:, at] = f(u4, 0) + f(q1, 0) + f(q2, 0) + f(q3, 0)
            s4[:, at] = (f(u4, 1) + f(q1, 1) + f(q2, 1) + f(q3, 1)).astype(jnp.bfloat16)

        @pl.when(core == 1)
        def _():
            keep[:, at] = f(u3, 0) + f(q1, 0)
            s4[:, at] = (f(u3, 1) + f(q1, 1)).astype(jnp.bfloat16)
            s5[:, at] = (f(u4, 0) + f(q2, 0)).astype(jnp.bfloat16)
            s6[:, at] = (f(u4, 1) + f(q2, 1)).astype(jnp.bfloat16)


def stage_sum(terms):
    parts = len(terms)
    _, rows, cols = terms[0][0].shape
    one = jax.ShapeDtypeStruct((rows, parts * cols), jnp.bfloat16)
    return pl.pallas_call(
        functools.partial(stage_body, parts),
        in_specs=[VM] * (5 * parts),
        out_specs=[VM] * 4,
        out_shape=[jax.ShapeDtypeStruct(one.shape, jnp.float32), one, one, one],
        cost_estimate=cost(1),
        compiler_params=params(4),
        name="stage_sum",
    )(*[x for t in terms for x in t])


def last_body(keep, q4, q5, q6, out):
    core = lax.axis_index("c")

    @pl.when(core == 0)
    def _():
        out[...] = (keep[...] + q4[...].astype(jnp.float32)).astype(jnp.bfloat16)

    @pl.when(core == 1)
    def _():
        total = keep[...] + q4[...].astype(jnp.float32)
        total += q5[...].astype(jnp.float32) + q6[...].astype(jnp.float32)
        out[...] = total.astype(jnp.bfloat16)


def last_sum(keep, q4, q5, q6):
    return pl.pallas_call(
        last_body,
        in_specs=[VM] * 4,
        out_specs=VM,
        out_shape=jax.ShapeDtypeStruct(q4.shape, q4.dtype),
        cost_estimate=cost(1),
        compiler_params=params(4),
        name="last_sum",
    )(keep, q4, q5, q6)


def gather(own):
    r1 = move(own, X, Y1)
    r2 = move(own, Y1, Y2)
    r3 = move(own, Y3, Y3)
    r4 = move(own, Y2, X)
    r5 = move(r1, Y1, X)
    r6 = move(pick(r1, r2), Y3, X)
    r7 = move(pick(r1, r3), Y2, X)
    return [own, r1, r2, r3, r4, r5, r6, r7]


def scatter(halves):
    terms = []
    for mine, came in halves:
        u1, u2, u3, u4 = chip_sum(mine, came)
        q1 = move(u1, Y1, X)
        q2 = move(u2, Y3, X)
        q3 = move(u3, Y2, None)
        terms.append((u3, u4, q1, q2, q3))
    keep, s4, s5, s6 = stage_sum(terms)
    q4 = move(s4, X, Y1)
    q5 = move(s5, None, Y3)
    q6 = move(s6, None, Y2)
    return last_sum(keep, q4, q5, q6)


def body(codes, exps, wavefield, observed, mask):
    _, rows, cols = codes.shape
    own = wavefield.transpose(0, 2, 1).reshape(16, cols)
    pieces = gather(own)
    wide, seen = prepare(exps.T, observed)
    pieces += [swap(p) for p in pieces]
    parts = forward(pieces, codes, wide)
    parts = lax.all_to_all(parts, SRC, 0, 0, tiled=True)
    every, own_resid = residual(parts, vmem(seen), mask.reshape(1, rows))
    every = lax.all_to_all(every, SRC, 0, 0, tiled=True)
    halves = []
    for p in range(2):
        other, *mine = backward(every, codes, wide, p, 2)
        halves.append((mine, swap(other)))
    gradient = scatter(halves)
    gradient = gradient.reshape(2, 8, cols)
    return own_resid.reshape(2, 16, rows).transpose(0, 2, 1), gradient.transpose(0, 2, 1)


def solution(mesh):
    fine = Mesh(mesh.devices.reshape(2, 4, 2, 4, 2), ("xh", "y", "c", "z", "xl"))
    in_specs = (P(None, RCV, SRC), P(RCV, SRC), P(None, SRC, RCV), P(None, RCV, None), P(RCV))
    out_specs = (P(None, RCV, SRC), P(None, SRC, RCV))
    return jax.shard_map(body, mesh=fine, in_specs=in_specs, out_specs=out_specs, check_vma=False)
```
